32 devices in a mesh: harm: 4 (over y, x), slab: 8 (over z, core).
Axes of the slice: x: 2, y: 2, z: 4, core: 2. Of those that a mesh axis runs over, the one named last changes fastest.
Arguments:
- krylov_basis: float32 [3, 4, 4, 16, 32, 128], P(None, 'harm', None, 'slab'), may hold values from -16 to 16
- weights: float32 [3], replicated, may hold values from -3 to 3
- base_flow: bfloat16 [4, 3, 16, 32, 128], P('harm', None, 'slab'), may hold values from -4 to 4
- shifts: float32 [4], P('harm'), may hold values from 0.25 to 2
Outputs:
- next_vector: float32 [4, 4, 16, 32, 128], P('harm', None, 'slab')
- arnoldi_column: float32 [4], replicated
The draws below stay inside these ranges and needn't reach their ends.
All inputs are finite; a program needn't handle non-finite values.
Results may differ from the reference program's by a relative error of at most 0.009.
Values may be sent and summed in bfloat16 or wider, within the bound.
No kernel may reach another device: no remote copies, remote signals or barrier semaphores. Data moves between devices by JAX's collectives and lax.ppermute only.
A program may use at most 64 MiB of HBM per device.

```python
import math
import jax
import jax.numpy as jnp
from jax import lax

F = 4
NY = 32
NZ = 128
SWEEPS = 4
BASIS = 3
H = 4
NX = 16


def draw_krylov_basis(key, part):
    first_key = jax.random.fold_in(jax.random.fold_in(key, 11), 0)
    full_shape = (BASIS, H, F, NX, NY, NZ)
    along_x = (jnp.arange(NX, dtype=jnp.float32) / max(NX - 1, 1)).reshape(1, 1, 1, NX, 1, 1)
    along_h = (jnp.arange(H, dtype=jnp.float32) / max(H - 1, 1)).reshape(1, H, 1, 1, 1, 1)
    energy = jnp.power(10.0, 0.5 * (along_x + along_h)) / 3.527
    values = jax.random.truncated_normal(first_key, -6.0, 6.0, full_shape, jnp.float32)
    return values * jnp.sqrt(energy)


def levels(own_key, extent, cuts, least, top_value):
    factor_of, own = 1.0, jax.random.fold_in(own_key, 6)
    for axis_at, blocks in cuts:
        steps = jnp.exp(jax.random.uniform(jax.random.fold_in(own, axis_at), (blocks,), jnp.float32, least / len(cuts), top_value / len(cuts)))
        factor_of = factor_of * jnp.repeat(steps, extent[axis_at] // blocks).reshape([-1 if axis == axis_at else 1 for axis in range(len(extent))])
    return factor_of


def normal_values(stream_key, dims, scale, most, shards=(), held_as=jnp.bfloat16):
    drawn = jax.random.normal(stream_key, dims, jnp.float32) * scale
    if len(shards) > 0:
        drawn = levels(stream_key, dims, shards, -0.22, 0.18) * drawn
    return jnp.clip(drawn, min=-most, max=most).astype(held_as)


def setup_inputs(seed: int = 0) -> dict:
    key_of = jax.random.split(jax.random.key(seed), 5)
    krylov_basis = draw_krylov_basis(jax.random.fold_in(key_of[4], 71), 0)
    weights = normal_values(key_of[1], (BASIS,), 1.0, 3.0, (), jnp.float32)
    base_flow = normal_values(key_of[2], (H, 3, NX, NY, NZ), 1.0, 4.0, ((0, 4), (2, 8)))
    shifts = jnp.clip(jnp.exp(math.log(2.0) - 2.0794415 * jax.random.uniform(key_of[3], (H,), jnp.float32) ** levels(key_of[3], (H,), ((0, 4),), -0.2, 0.2)), 0.25, 2.0)
    return dict(krylov_basis=krylov_basis, weights=weights, base_flow=base_flow, shifts=shifts)


viscosity = 1.0
epsilon = 1e-06

def neighbours_y(values):
    padded = jnp.pad(values, ((0, 0), (0, 0), (1, 1), (0, 0)))
    return (padded[:, :, 2:], padded[:, :, :-2])

def laplace_ext(extended):
    center = extended[:, 1:-1]
    upper_y, lower_y = neighbours_y(center)
    result = extended[:, 2:] + extended[:, :-2] + upper_y + lower_y
    result = result + jnp.roll(center, -1, axis=3) + jnp.roll(center, 1, axis=3)
    return result - 6.0 * center

def divergence_ext(extended):
    flux_x = extended[0:4]
    flux_y = extended[4:8, 1:-1]
    flux_z = extended[8:12, 1:-1]
    upper_y, lower_y = neighbours_y(flux_y)
    result = 0.5 * (flux_x[:, 2:] - flux_x[:, :-2])
    result = result + 0.5 * (upper_y - lower_y)
    return result + 0.5 * (jnp.roll(flux_z, -1, axis=3) - jnp.roll(flux_z, 1, axis=3))

def pad_planes(values):
    return jnp.pad(values, ((0, 0), (1, 1), (0, 0), (0, 0)))

def chebyshev(applied, shift_value, extend):
    middle = shift_value + 6.0 * viscosity
    half_span = 6.0 * viscosity
    span_ratio = middle / half_span
    solution = jnp.zeros_like(applied)
    remainder = applied
    direction = applied / middle
    ratio_prev = 1.0 / span_ratio
    for sweep_index in range(SWEEPS):
        solution = solution + direction
        remainder = remainder - (shift_value * direction - viscosity * laplace_ext(extend(direction)))
        ratio_next = 1.0 / (2.0 * span_ratio - ratio_prev)
        direction = ratio_next * ratio_prev * direction + 2.0 * ratio_next / half_span * remainder
        ratio_prev = ratio_next
    return solution + direction

def reference(krylov_basis, weights, base_flow, shifts):
    start_vec = lax.optimization_barrier(jnp.sum(weights[:, None, None, None, None, None] * krylov_basis, axis=0))
    mean_flow = base_flow.astype(jnp.float32)
    harm_ids = jnp.arange(H, dtype=jnp.int32)

    def one_harmonic(harmonic):

        def add_pair(partner, running):
            flow_row = ((harmonic - partner) % H).astype(jnp.int32)
            flow_part = lax.dynamic_index_in_dim(mean_flow, flow_row, 0, keepdims=False)
            source = lax.dynamic_index_in_dim(start_vec, partner, 0, keepdims=False)
            return running + flow_part[:, None] * source[None]
        fluxes = lax.fori_loop(0, H, add_pair, jnp.zeros((3, F, NX, NY, NZ), jnp.float32))
        fluxes = fluxes.reshape(3 * F, NX, NY, NZ)
        own_field = lax.dynamic_index_in_dim(start_vec, harmonic, 0, keepdims=False)
        own_shift = lax.dynamic_index_in_dim(shifts, harmonic, 0, keepdims=False)
        applied = own_shift * own_field - viscosity * laplace_ext(pad_planes(own_field))
        applied = applied + divergence_ext(pad_planes(fluxes))
        return chebyshev(applied, own_shift, pad_planes)
    solution = lax.map(one_harmonic, harm_ids)
    entries = float(H * F * NX * NY * NZ)
    projection = jnp.stack([jnp.sum(krylov_basis[member] * solution) for member in range(BASIS)]) / entries
    residue = solution
    for member in range(BASIS):
        residue = residue - projection[member] * krylov_basis[member]
    norm_value = jnp.sqrt(jnp.sum(residue * residue) / entries + epsilon)
    next_vector = residue / norm_value
    arnoldi_column = jnp.concatenate([projection, norm_value[None]])
    return (next_vector, arnoldi_column)
```

```python
import math

import jax
import jax.numpy as jnp
from jax import lax
from jax.experimental import pallas as pl
from jax.experimental.pallas import tpu as pltpu
from jax.sharding import PartitionSpec as P

SWEEPS = 4
DIRS = 3
VISCOSITY = 1.0
EPSILON = 1e-06
BASIS_MAX, WEIGHT_MAX, FLOW_MAX, SHIFT_MAX = 16.0, 3.0, 4.0, 2.0
SENT_MAX = 60000.0
F32 = jnp.float32
SENT = jnp.float16
VMEM = pl.BlockSpec(memory_space=pltpu.VMEM)
SMEM = pl.BlockSpec(memory_space=pltpu.SMEM)


def call(body, out_shape, args, specs, out_specs, scratch=()):
    return pl.pallas_call(
        body, out_shape=out_shape, in_specs=specs, out_specs=out_specs, scratch_shapes=scratch,
        compiler_params=pltpu.CompilerParams(vmem_limit_bytes=8 << 20),
    )(*args)


def rows(shape):
    return lax.broadcasted_iota(jnp.int32, shape, len(shape) - 2)


def y_up(plane):
    count = plane.shape[-2]
    return jnp.where(rows(plane.shape) < count - 1, pltpu.roll(plane, count - 1, plane.ndim - 2), 0.0)


def y_down(plane):
    return jnp.where(rows(plane.shape) > 0, pltpu.roll(plane, 1, plane.ndim - 2), 0.0)


def z_up(plane):
    return pltpu.roll(plane, plane.shape[-1] - 1, plane.ndim - 1)


def z_down(plane):
    return pltpu.roll(plane, 1, plane.ndim - 1)


def parity():
    return lax.rem(lax.axis_index("slab"), 2)


def scales(count, harmonics):
    vector = count * WEIGHT_MAX * BASIS_MAX
    flux = harmonics * FLOW_MAX * vector
    applied = (SHIFT_MAX + 12.0 * VISCOSITY) * vector + DIRS * flux
    return [2.0 ** math.floor(math.log2(SENT_MAX / bound)) for bound in (vector, applied)]


def start_kernel(basis_in, weights_in, flow_in, basis, vec, message, weights, flow, sems, *, rescale):
    count, fields = basis.shape[0], basis.shape[2]
    copies = [pltpu.make_async_copy(weights_in, weights, sems.at[0])]
    copies.append(pltpu.make_async_copy(flow_in, flow, sems.at[1]))
    copies += [pltpu.make_async_copy(basis_in.at[j], basis.at[j], sems.at[2 + j]) for j in range(count)]
    for copy in copies:
        copy.start()
    for copy in copies:
        copy.wait()
    for f in range(fields):
        total = weights[0] * basis[0, 0, f]
        for j in range(1, count):
            total = total + weights[j] * basis[j, 0, f]
        vec[f] = total
        message[f] = total * rescale
    message[fields:] = flow[0].astype(F32)


def gram_kernel(basis, sums):
    count = basis.shape[0]
    lanes = lax.broadcasted_iota(jnp.int32, sums.shape, 1)
    line, place = jnp.zeros(sums.shape, F32), 1 + count
    for i in range(count):
        for j in range(i, count):
            line = jnp.where(lanes == place, jnp.sum(basis[i, 0] * basis[j, 0]), line)
            place += 1
    sums[...] = line


def flux_kernel(shift, vec, *refs, harmonics, unscale, rescale):
    messages = refs[:harmonics]
    partial, away, away_sent, flows = refs[harmonics:]
    fields, planes = vec.shape[0], vec.shape[1]
    harm = lax.axis_index("harm")
    core = parity()
    sign = 0.5 * (1 - 2 * core).astype(F32)
    flip = core == 1
    for j in range(harmonics):
        flow = messages[0][...].astype(F32) if j == 0 else messages[j][fields:]
        flows[lax.rem(harm - j + harmonics, harmonics)] = flow
    own = shift[0] + 6.0 * VISCOSITY
    for f in range(fields):
        local, plus, minus = [], [], []
        for t in range(planes):
            x = jnp.where(flip, planes - 1 - t, t)
            center = vec[f, x]
            flux = [flows[0, d, x] * center for d in range(DIRS)]
            for j in range(1, harmonics):
                other = messages[j][f, x] * unscale
                flux = [flux[d] + flows[j, d, x] * other for d in range(DIRS)]
            half_y = 0.5 * flux[1]
            half_z = 0.5 * flux[2]
            half_x = sign * flux[0]
            value = own * center + y_up(half_y - VISCOSITY * center) - y_down(half_y + VISCOSITY * center)
            value = value + z_up(half_z - VISCOSITY * center) - z_down(half_z + VISCOSITY * center)
            local.append(value)
            plus.append(half_x - VISCOSITY * center)
            minus.append(-half_x - VISCOSITY * center)
        for t in range(planes):
            value = local[t]
            if t + 1 < planes:
                value = value + plus[t + 1]
            if t > 0:
                value = value + minus[t - 1]
            partial[t, f] = value
        partial[planes, f] = minus[planes - 1]
        away[f] = plus[0]
        away_sent[f] = plus[0] * rescale


def chip_kernel(mine, theirs, away, message, *, rescale):
    planes = mine.shape[0] - 1
    for t in range(planes):
        own, other = mine[t], theirs[planes - 1 - t]
        if t == planes - 1:
            own = own + theirs[planes]
        if t == 0:
            other = other + mine[planes]
        message[t] = own * rescale
        message[planes + t] = other * rescale
    message[2 * planes] = away[...] * rescale


def inner_kernel(mine, theirs, away, outer, message, *, unscale):
    planes = mine.shape[0] - 1
    message[0] = outer[0] * unscale + away[...]
    for t in range(1, planes):
        message[t] = outer[t] * unscale
    own = mine[0] + outer[2 * planes] * unscale
    if planes == 1:
        own = own + theirs[planes]
    message[planes] = own


def chebyshev_kernel(shift, gram, basis, vec, mine, theirs, away, outer, inner, far, change, sums, *, unscale):
    count, fields = basis.shape[0], vec.shape[0]
    planes = mine.shape[0] - 1
    slab, slabs = lax.axis_index("slab"), lax.axis_size("slab")
    core = parity()
    flip = core == 1
    chip, chips = lax.div(slab, 2), slabs // 2
    has_low = (chip > 0).astype(F32)
    has_high = (chip < chips - 1).astype(F32)
    has_outer = jnp.where(flip, has_high, has_low)
    has_inner = jnp.where(flip, has_low, has_high)
    two_away = jnp.where(flip, chips - 1 - chip, chip) > 1
    has_far = two_away.astype(F32)
    own_shift = shift[0]
    middle = own_shift + 6.0 * VISCOSITY
    half_span = 6.0 * VISCOSITY
    span_ratio = middle / half_span
    ratio = 1.0 / span_ratio
    gains, far_gain = [], 1.0 / middle
    for _ in range(SWEEPS):
        following = 1.0 / (2.0 * span_ratio - ratio)
        gains.append((following * ratio, 2.0 * following / half_span))
        far_gain = far_gain * (gains[-1][1] * VISCOSITY)
        ratio = following
    depth = SWEEPS
    first = 1.0 / middle
    totals = [None] * (1 + count)
    for f in range(fields):
        remainder = [outer[depth - 1 - i, f] * unscale for i in range(depth - 1)]
        remainder.append(outer[0, f] * unscale + away[f])
        scale = [has_outer] * depth + [None] * (2 * planes) + [has_inner] * planes
        for t in range(planes):
            value = mine[t, f]
            if t == planes - 1:
                value = value + theirs[planes, f]
            if t == 0:
                value = value + outer[2 * planes, f] * unscale
            remainder.append(value)
        for t in range(planes - 1, -1, -1):
            if t == 0:
                remainder.append(inner[planes, f])
            elif t == planes - 1:
                remainder.append(theirs[t, f] + mine[planes, f])
            else:
                remainder.append(theirs[t, f])
        for t in range(planes):
            remainder.append(inner[t, f])
        direction = [
            (r * first) if m is None else (r * (first * m)) for r, m in zip(remainder, scale)
        ]
        solution = [direction[depth + t] for t in range(planes)]
        low = 0
        for sweep in range(SWEEPS):
            keep, gain = gains[sweep]
            nothing = low + 1
            end = low + len(direction) - 1
            next_remainder, next_direction = [], []
            for position in range(nothing, end):
                i = position - low
                d = direction[i]
                around = direction[i + 1] + direction[i - 1] + y_up(d) + y_down(d) + z_up(d) + z_down(d)
                r = remainder[i] - (middle * d - VISCOSITY * around)
                m = scale[position]
                if m is None:
                    n = keep * d + gain * r
                else:
                    n = (keep * m) * d + (gain * m) * r
                next_remainder.append(r)
                next_direction.append(n)
            remainder, direction, low = next_remainder, next_direction, low + 1
            solution = [s + direction[depth - low + t] for t, s in enumerate(solution)]
        solution[0] = solution[0] + (far_gain * unscale * has_far) * far[f]
        for t in range(planes):
            x = jnp.where(flip, planes - 1 - t, t)
            moved = solution[t] - vec[f, x]
            change[f, x] = moved
            parts = [moved * moved] + [basis[j, 0, f, x] * moved for j in range(count)]
            totals = [p if q is None else q + p for q, p in zip(totals, parts)]
    lanes = lax.broadcasted_iota(jnp.int32, (1, sums.shape[-1]), 1)
    line = gram[...]
    place = 0
    for total in totals:
        line = jnp.where(lanes == place, jnp.sum(total), line)
        place += 1
    sums[...] = jnp.broadcast_to(line[None], sums.shape)


def final_kernel(weights, basis, change, sums, vector, column, *, entries):
    count = basis.shape[0]
    line = jnp.sum(sums[:, 0, :], axis=0, keepdims=True) * (1.0 / entries)
    lanes = lax.broadcasted_iota(jnp.int32, line.shape, 1)

    def entry(place):
        return jnp.sum(jnp.where(lanes == place, line, 0.0))

    square = entry(0)
    moved = [entry(1 + j) for j in range(count)]
    gram, place = {}, 1 + count
    for i in range(count):
        for j in range(i, count):
            gram[i, j] = gram[j, i] = entry(place)
            place += 1
    projection, excess = [], []
    for j in range(count):
        value = moved[j]
        for i in range(count):
            value = value + weights[i] * gram[i, j]
        projection.append(value)
        excess.append(value - weights[j])
    for j in range(count):
        inner = -2.0 * moved[j]
        for i in range(count):
            inner = inner + excess[i] * gram[i, j]
        square = square + excess[j] * inner
    norm = jnp.sqrt(jnp.full((1, line.shape[-1]), jnp.maximum(square, 0.0) + EPSILON, F32))
    inverse = (1.0 / norm)[:, None, None, :]
    residue = change[...]
    for j in range(count):
        residue = residue - excess[j] * basis[j, 0]
    vector[0] = residue * inverse
    for j in range(count):
        column[j] = projection[j]
    column[count] = jnp.max(norm)


def shards(krylov_basis, weights, base_flow, shifts):
    count, _, fields, planes, ny, nz = krylov_basis.shape
    harmonics, slabs = lax.axis_size("harm"), lax.axis_size("slab")
    assert 2 * planes == SWEEPS and slabs % 2 == 0
    shape = (fields, planes, ny, nz)
    vec_scale, applied_scale = scales(count, harmonics)

    def start_body(*refs):
        start_kernel(*refs, rescale=vec_scale)

    basis, vec, message = call(
        start_body,
        [
            jax.ShapeDtypeStruct(krylov_basis.shape, F32),
            jax.ShapeDtypeStruct(shape, F32),
            jax.ShapeDtypeStruct((fields + DIRS, planes, ny, nz), F32),
        ],
        [pltpu.with_memory_space_constraint(x, pltpu.HBM) for x in (krylov_basis, weights, base_flow)],
        [pl.BlockSpec(memory_space=pltpu.HBM)] * 3,
        [VMEM] * 3,
        [
            pltpu.SMEM(weights.shape, F32),
            pltpu.VMEM(base_flow.shape, base_flow.dtype),
            pltpu.SemaphoreType.DMA((2 + count,)),
        ],
    )
    message = message.astype(SENT)
    gram = call(gram_kernel, jax.ShapeDtypeStruct((1, nz), F32), (basis,), [VMEM], VMEM)
    messages = [base_flow[0]] + [
        lax.ppermute(message, "harm", [(i, (i + j) % harmonics) for i in range(harmonics)]).astype(F32)
        for j in range(1, harmonics)
    ]

    def flux_body(*refs):
        flux_kernel(*refs, harmonics=harmonics, unscale=1.0 / vec_scale, rescale=applied_scale)

    mine, away, away_sent = call(
        flux_body,
        [
            jax.ShapeDtypeStruct((planes + 1, fields, ny, nz), F32),
            jax.ShapeDtypeStruct((fields, ny, nz), F32),
            jax.ShapeDtypeStruct((fields, ny, nz), F32),
        ],
        (shifts, vec, *messages),
        [SMEM] + [VMEM] * (1 + harmonics),
        [VMEM] * 3,
        [pltpu.VMEM((harmonics, DIRS, planes, ny, nz), F32)],
    )
    swap = [(i, i ^ 1) for i in range(slabs)]
    links = [(i, i + 1) for i in range(1, slabs - 1, 2)]
    cross = links + [(b, a) for a, b in links]
    skips = [(i, i + 3) for i in range(1, slabs - 3, 2)]
    beyond = skips + [(b, a) for a, b in skips]
    theirs = lax.ppermute(mine, "slab", swap)

    def chip_body(*refs):
        chip_kernel(*refs, rescale=applied_scale)

    chip = call(
        chip_body,
        jax.ShapeDtypeStruct((2 * planes + 1, fields, ny, nz), F32),
        (mine, theirs, away),
        [VMEM] * 3,
        VMEM,
    )
    outer = lax.ppermute(chip.astype(SENT), "slab", cross).astype(F32)
    masks = {a ^ b for a, b in beyond}
    if len(masks) == 1 and slabs & (slabs - 1) == 0:
        beyond = [(i, i ^ mask) for i in range(slabs) for mask in masks]
    far = lax.ppermute(away_sent.astype(SENT), "slab", beyond).astype(F32)

    outer, far = lax.optimization_barrier((outer, far))

    def inner_body(*refs):
        inner_kernel(*refs, unscale=1.0 / applied_scale)

    held = call(
        inner_body,
        jax.ShapeDtypeStruct((planes + 1, fields, ny, nz), F32),
        (mine, theirs, away, outer),
        [VMEM] * 4,
        VMEM,
    )
    inner = lax.ppermute(held, "slab", swap)
    devices = harmonics * slabs

    def chebyshev_body(*refs):
        chebyshev_kernel(*refs, unscale=1.0 / applied_scale)

    change, sums = call(
        chebyshev_body,
        [jax.ShapeDtypeStruct(shape, F32), jax.ShapeDtypeStruct((devices, 1, nz), F32)],
        (shifts, gram, basis, vec, mine, theirs, away, outer, inner, far),
        [SMEM] + [VMEM] * 9,
        [VMEM, VMEM],
    )
    sums = lax.all_to_all(sums, ("harm", "slab"), 0, 0, tiled=True)
    entries = float(devices * fields * planes * ny * nz)

    def final_body(*refs):
        final_kernel(*refs, entries=entries)

    vector, column = call(
        final_body,
        [jax.ShapeDtypeStruct((1,) + shape, F32), jax.ShapeDtypeStruct((count + 1,), F32)],
        (weights, basis, change, sums),
        [SMEM] + [VMEM] * 3,
        [VMEM, SMEM],
    )
    return vector, column


def solution(mesh):
    in_specs = (
        P(None, "harm", None, "slab", None, None),
        P(),
        P("harm", None, "slab", None, None),
        P("harm"),
    )
    out_specs = (P("harm", None, "slab", None, None), P())
    return jax.shard_map(shards, mesh=mesh, in_specs=in_specs, out_specs=out_specs, check_vma=False)
```

```python
import math

import jax
import jax.numpy as jnp
from jax import lax
from jax.experimental import pallas as pl
from jax.experimental.pallas import tpu as pltpu
from jax.sharding import PartitionSpec as P

SWEEPS = 4
DIRS = 3
VISCOSITY = 1.0
EPSILON = 1e-06
BASIS_MAX, WEIGHT_MAX, FLOW_MAX, SHIFT_MAX = 16.0, 3.0, 4.0, 2.0
SENT_MAX = 60000.0
F32 = jnp.float32
SENT = jnp.float16
VMEM = pl.BlockSpec(memory_space=pltpu.VMEM)
SMEM = pl.BlockSpec(memory_space=pltpu.SMEM)


def call(body, out_shape, args, specs, out_specs, scratch=()):
    return pl.pallas_call(
        body, out_shape=out_shape, in_specs=specs, out_specs=out_specs, scratch_shapes=scratch,
        compiler_params=pltpu.CompilerParams(vmem_limit_bytes=8 << 20),
    )(*args)


def rows(shape):
    return lax.broadcasted_iota(jnp.int32, shape, len(shape) - 2)


def y_up(plane):
    count = plane.shape[-2]
    return jnp.where(rows(plane.shape) < count - 1, pltpu.roll(plane, count - 1, plane.ndim - 2), 0.0)


def y_down(plane):
    return jnp.where(rows(plane.shape) > 0, pltpu.roll(plane, 1, plane.ndim - 2), 0.0)


def z_up(plane):
    return pltpu.roll(plane, plane.shape[-1] - 1, plane.ndim - 1)


def z_down(plane):
    return pltpu.roll(plane, 1, plane.ndim - 1)


def parity():
    return lax.rem(lax.axis_index("slab"), 2)


def scales(count, harmonics):
    vector = count * WEIGHT_MAX * BASIS_MAX
    flux = harmonics * FLOW_MAX * vector
    applied = (SHIFT_MAX + 12.0 * VISCOSITY) * vector + DIRS * flux
    return [2.0 ** math.floor(math.log2(SENT_MAX / bound)) for bound in (vector, applied)]


def start_kernel(basis_in, weights_in, flow_in, basis, vec, message, scalars, weights, flow, sems, *, rescale):
    count, fields = basis.shape[0], basis.shape[2]
    copies = [pltpu.make_async_copy(weights_in, weights, sems.at[0])]
    copies.append(pltpu.make_async_copy(flow_in, flow, sems.at[1]))
    copies += [pltpu.make_async_copy(basis_in.at[j], basis.at[j], sems.at[2 + j]) for j in range(count)]
    for copy in copies:
        copy.start()
    for copy in copies:
        copy.wait()
    for f in range(fields):
        total = weights[0] * basis[0, 0, f]
        for j in range(1, count):
            total = total + weights[j] * basis[j, 0, f]
        vec[f] = total
        message[f] = total * rescale
    message[fields:] = flow[0].astype(F32)
    for j in range(count):
        scalars[j : j + 1] = jnp.full((1, scalars.shape[1]), weights[j], F32)


def gram_kernel(basis, sums):
    count = basis.shape[0]
    lanes = lax.broadcasted_iota(jnp.int32, sums.shape, 1)
    line, place = jnp.zeros(sums.shape, F32), 1 + count
    for i in range(count):
        for j in range(i, count):
            line = jnp.where(lanes == place, jnp.sum(basis[i, 0] * basis[j, 0]), line)
            place += 1
    sums[...] = line


def flux_kernel(shift, vec, *refs, harmonics, unscale, rescale):
    messages = refs[:harmonics]
    partial, away, away_sent, flows = refs[harmonics:]
    fields, planes = vec.shape[0], vec.shape[1]
    harm = lax.axis_index("harm")
    core = parity()
    sign = 0.5 * (1 - 2 * core).astype(F32)
    flip = core == 1
    for j in range(harmonics):
        flows[lax.rem(harm - j + harmonics, harmonics)] = messages[j][fields:]
    own = shift[...] + 6.0 * VISCOSITY
    for f in range(fields):
        local, plus, minus = [], [], []
        for t in range(planes):
            x = jnp.where(flip, planes - 1 - t, t)
            center = vec[f, x]
            flux = [flows[0, d, x] * center for d in range(DIRS)]
            for j in range(1, harmonics):
                other = messages[j][f, x] * unscale
                flux = [flux[d] + flows[j, d, x] * other for d in range(DIRS)]
            half_y = 0.5 * flux[1]
            half_z = 0.5 * flux[2]
            half_x = sign * flux[0]
            value = own * center + y_up(half_y - VISCOSITY * center) - y_down(half_y + VISCOSITY * center)
            value = value + z_up(half_z - VISCOSITY * center) - z_down(half_z + VISCOSITY * center)
            local.append(value)
            plus.append(half_x - VISCOSITY * center)
            minus.append(-half_x - VISCOSITY * center)
        for t in range(planes):
            value = local[t]
            if t + 1 < planes:
                value = value + plus[t + 1]
            if t > 0:
                value = value + minus[t - 1]
            partial[t, f] = value
        partial[planes, f] = minus[planes - 1]
        away[f] = plus[0]
        away_sent[f] = plus[0] * rescale


def chip_kernel(mine, theirs, away, message, *, rescale):
    planes = mine.shape[0] - 1
    for t in range(planes):
        own, other = mine[t], theirs[planes - 1 - t]
        if t == planes - 1:
            own = own + theirs[planes]
        if t == 0:
            other = other + mine[planes]
        message[t] = own * rescale
        message[planes + t] = other * rescale
    message[2 * planes] = away[...] * rescale


def inner_kernel(mine, theirs, away, outer, message, *, unscale):
    planes = mine.shape[0] - 1
    message[0] = outer[0] * unscale + away[...]
    for t in range(1, planes):
        message[t] = outer[t] * unscale
    own = mine[0] + outer[2 * planes] * unscale
    if planes == 1:
        own = own + theirs[planes]
    message[planes] = own


def chebyshev_kernel(shift, gram, basis, vec, mine, theirs, away, outer, inner, far, change, sums, *, unscale):
    count, fields = basis.shape[0], vec.shape[0]
    planes = mine.shape[0] - 1
    slab, slabs = lax.axis_index("slab"), lax.axis_size("slab")
    core = parity()
    flip = core == 1
    chip, chips = lax.div(slab, 2), slabs // 2
    has_low = (chip > 0).astype(F32)
    has_high = (chip < chips - 1).astype(F32)
    has_outer = jnp.where(flip, has_high, has_low)
    has_inner = jnp.where(flip, has_low, has_high)
    two_away = jnp.where(flip, chips - 1 - chip, chip) > 1
    has_far = two_away.astype(F32)
    own_shift = shift[...]
    middle = own_shift + 6.0 * VISCOSITY
    half_span = 6.0 * VISCOSITY
    span_ratio = middle / half_span
    ratio = 1.0 / span_ratio
    gains, far_gain = [], 1.0 / middle
    for _ in range(SWEEPS):
        following = 1.0 / (2.0 * span_ratio - ratio)
        gains.append((following * ratio, 2.0 * following / half_span))
        far_gain = far_gain * (gains[-1][1] * VISCOSITY)
        ratio = following
    depth = SWEEPS
    first = 1.0 / middle
    totals = [None] * (1 + count)
    for f in range(fields):
        remainder = [outer[depth - 1 - i, f] * unscale for i in range(depth - 1)]
        remainder.append(outer[0, f] * unscale + away[f])
        scale = [has_outer] * depth + [None] * (2 * planes) + [has_inner] * planes
        for t in range(planes):
            value = mine[t, f]
            if t == planes - 1:
                value = value + theirs[planes, f]
            if t == 0:
                value = value + outer[2 * planes, f] * unscale
            remainder.append(value)
        for t in range(planes - 1, -1, -1):
            if t == 0:
                remainder.append(inner[planes, f])
            elif t == planes - 1:
                remainder.append(theirs[t, f] + mine[planes, f])
            else:
                remainder.append(theirs[t, f])
        for t in range(planes):
            remainder.append(inner[t, f])
        direction = [
            (r * first) if m is None else (r * (first * m)) for r, m in zip(remainder, scale)
        ]
        solution = [direction[depth + t] for t in range(planes)]
        low = 0
        for sweep in range(SWEEPS):
            keep, gain = gains[sweep]
            nothing = low + 1
            end = low + len(direction) - 1
            next_remainder, next_direction = [], []
            for position in range(nothing, end):
                i = position - low
                d = direction[i]
                around = direction[i + 1] + direction[i - 1] + y_up(d) + y_down(d) + z_up(d) + z_down(d)
                r = remainder[i] - (middle * d - VISCOSITY * around)
                m = scale[position]
                if m is None:
                    n = keep * d + gain * r
                else:
                    n = (keep * m) * d + (gain * m) * r
                next_remainder.append(r)
                next_direction.append(n)
            remainder, direction, low = next_remainder, next_direction, low + 1
            solution = [s + direction[depth - low + t] for t, s in enumerate(solution)]
        solution[0] = solution[0] + (far_gain * unscale * has_far) * far[f]
        for t in range(planes):
            x = jnp.where(flip, planes - 1 - t, t)
            moved = solution[t] - vec[f, x]
            change[f, x] = moved
            parts = [moved * moved] + [basis[j, 0, f, x] * moved for j in range(count)]
            totals = [p if q is None else q + p for q, p in zip(totals, parts)]
    lanes = lax.broadcasted_iota(jnp.int32, (1, sums.shape[-1]), 1)
    line = gram[...]
    place = 0
    for total in totals:
        line = jnp.where(lanes == place, jnp.sum(total), line)
        place += 1
    sums[...] = jnp.broadcast_to(line[None], sums.shape)


def final_kernel(scalars, basis, change, sums, vector, column, *, entries):
    count = basis.shape[0]
    line = jnp.sum(sums[:, 0, :], axis=0, keepdims=True) * (1.0 / entries)
    lanes = lax.broadcasted_iota(jnp.int32, line.shape, 1)

    def entry(place):
        return jnp.sum(jnp.where(lanes == place, line, 0.0), axis=1, keepdims=True)

    square = entry(0)
    moved = [entry(1 + j) for j in range(count)]
    gram, place = {}, 1 + count
    for i in range(count):
        for j in range(i, count):
            gram[i, j] = gram[j, i] = entry(place)
            place += 1
    weights = [scalars[j : j + 1] for j in range(count)]
    projection, excess = [], []
    for j in range(count):
        value = moved[j]
        for i in range(count):
            value = value + weights[i] * gram[i, j]
        projection.append(value)
        excess.append(value - weights[j])
    for j in range(count):
        inner = -2.0 * moved[j]
        for i in range(count):
            inner = inner + excess[i] * gram[i, j]
        square = square + excess[j] * inner
    norm = jnp.sqrt(jnp.maximum(square, 0.0) + EPSILON)
    inverse = (1.0 / norm)[:, None, None, :]
    residue = change[...]
    for j in range(count):
        residue = residue - excess[j][:, None, None, :] * basis[j, 0]
    vector[0] = residue * inverse
    for j in range(count):
        column[j] = jnp.max(projection[j])
    column[count] = jnp.max(norm)


def shards(krylov_basis, weights, base_flow, shifts):
    count, _, fields, planes, ny, nz = krylov_basis.shape
    harmonics, slabs = lax.axis_size("harm"), lax.axis_size("slab")
    assert 2 * planes == SWEEPS and slabs % 2 == 0
    shape = (fields, planes, ny, nz)
    vec_scale, applied_scale = scales(count, harmonics)

    def start_body(*refs):
        start_kernel(*refs, rescale=vec_scale)

    basis, vec, message, scalars = call(
        start_body,
        [
            jax.ShapeDtypeStruct(krylov_basis.shape, F32),
            jax.ShapeDtypeStruct(shape, F32),
            jax.ShapeDtypeStruct((fields + DIRS, planes, ny, nz), F32),
            jax.ShapeDtypeStruct((count, nz), F32),
        ],
        [*(pltpu.with_memory_space_constraint(x, pltpu.HBM) for x in (krylov_basis, weights, base_flow))],
        [pl.BlockSpec(memory_space=pltpu.HBM)] * 3,
        [VMEM] * 4,
        [
            pltpu.SMEM(weights.shape, F32),
            pltpu.VMEM(base_flow.shape, base_flow.dtype),
            pltpu.SemaphoreType.DMA((2 + count,)),
        ],
    )
    whole, message = message, message.astype(SENT)
    shift = jnp.broadcast_to(shifts[:, None], (1, nz))
    gram = call(gram_kernel, jax.ShapeDtypeStruct((1, nz), F32), (basis,), [VMEM], VMEM)
    messages = [whole] + [
        lax.ppermute(message, "harm", [(i, (i + j) % harmonics) for i in range(harmonics)]).astype(F32)
        for j in range(1, harmonics)
    ]

    def flux_body(*refs):
        flux_kernel(*refs, harmonics=harmonics, unscale=1.0 / vec_scale, rescale=applied_scale)

    mine, away, away_sent = call(
        flux_body,
        [
            jax.ShapeDtypeStruct((planes + 1, fields, ny, nz), F32),
            jax.ShapeDtypeStruct((fields, ny, nz), F32),
            jax.ShapeDtypeStruct((fields, ny, nz), F32),
        ],
        (shift, vec, *messages),
        [VMEM] * (2 + harmonics),
        [VMEM] * 3,
        [pltpu.VMEM((harmonics, DIRS, planes, ny, nz), F32)],
    )
    swap = [(i, i ^ 1) for i in range(slabs)]
    links = [(i, i + 1) for i in range(1, slabs - 1, 2)]
    cross = links + [(b, a) for a, b in links]
    skips = [(i, i + 3) for i in range(1, slabs - 3, 2)]
    beyond = skips + [(b, a) for a, b in skips]
    theirs = lax.ppermute(mine, "slab", swap)

    def chip_body(*refs):
        chip_kernel(*refs, rescale=applied_scale)

    chip = call(
        chip_body,
        jax.ShapeDtypeStruct((2 * planes + 1, fields, ny, nz), F32),
        (mine, theirs, away),
        [VMEM] * 3,
        VMEM,
    )
    outer = lax.ppermute(chip.astype(SENT), "slab", cross).astype(F32)
    masks = {a ^ b for a, b in beyond}
    if len(masks) == 1 and slabs & (slabs - 1) == 0:
        beyond = [(i, i ^ mask) for i in range(slabs) for mask in masks]
    far = lax.ppermute(away_sent.astype(SENT), "slab", beyond).astype(F32)

    outer, far = lax.optimization_barrier((outer, far))

    def inner_body(*refs):
        inner_kernel(*refs, unscale=1.0 / applied_scale)

    held = call(
        inner_body,
        jax.ShapeDtypeStruct((planes + 1, fields, ny, nz), F32),
        (mine, theirs, away, outer),
        [VMEM] * 4,
        VMEM,
    )
    inner = lax.ppermute(held, "slab", swap)
    devices = harmonics * slabs

    def chebyshev_body(*refs):
        chebyshev_kernel(*refs, unscale=1.0 / applied_scale)

    change, sums = call(
        chebyshev_body,
        [jax.ShapeDtypeStruct(shape, F32), jax.ShapeDtypeStruct((devices, 1, nz), F32)],
        (shift, gram, basis, vec, mine, theirs, away, outer, inner, far),
        [VMEM] * 10,
        [VMEM, VMEM],
    )
    sums = lax.all_to_all(sums, ("harm", "slab"), 0, 0, tiled=True)
    entries = float(devices * fields * planes * ny * nz)

    def final_body(*refs):
        final_kernel(*refs, entries=entries)

    vector, column = call(
        final_body,
        [jax.ShapeDtypeStruct((1,) + shape, F32), jax.ShapeDtypeStruct((count + 1,), F32)],
        (scalars, basis, change, sums),
        [VMEM] * 4,
        [VMEM, SMEM],
    )
    return vector, column


def solution(mesh):
    in_specs = (
        P(None, "harm", None, "slab", None, None),
        P(),
        P("harm", None, "slab", None, None),
        P("harm"),
    )
    out_specs = (P("harm", None, "slab", None, None), P())
    return jax.shard_map(shards, mesh=mesh, in_specs=in_specs, out_specs=out_specs, check_vma=False)
```

```python
import math

import jax
import jax.numpy as jnp
from jax import lax
from jax.experimental import pallas as pl
from jax.experimental.pallas import tpu as pltpu
from jax.sharding import PartitionSpec as P


SWEEPS = 4
DIRS = 3
VISCOSITY = 1.0
EPSILON = 1e-06
BASIS_MAX, WEIGHT_MAX, FLOW_MAX, SHIFT_MAX = 16.0, 3.0, 4.0, 2.0
SENT_MAX = 60000.0
F32 = jnp.float32
SENT = jnp.float16
VMEM = pl.BlockSpec(memory_space=pltpu.VMEM)
SMEM = pl.BlockSpec(memory_space=pltpu.SMEM)


def call(body, out_shape, args, specs, out_specs, scratch=()):
    return pl.pallas_call(
        body, out_shape=out_shape, in_specs=specs, out_specs=out_specs, scratch_shapes=scratch,
        compiler_params=pltpu.CompilerParams(vmem_limit_bytes=8 << 20),
    )(*args)


def rows(shape):
    return lax.broadcasted_iota(jnp.int32, shape, len(shape) - 2)


def y_up(plane):
    count = plane.shape[-2]
    return jnp.where(rows(plane.shape) < count - 1, pltpu.roll(plane, count - 1, plane.ndim - 2), 0.0)


def y_down(plane):
    return jnp.where(rows(plane.shape) > 0, pltpu.roll(plane, 1, plane.ndim - 2), 0.0)


def z_up(plane):
    return pltpu.roll(plane, plane.shape[-1] - 1, plane.ndim - 1)


def z_down(plane):
    return pltpu.roll(plane, 1, plane.ndim - 1)


def parity():
    return lax.rem(lax.axis_index("slab"), 2)


def step(index, j, harmonics):
    if harmonics & (harmonics - 1) == 0:
        return index ^ j
    return (index + j) % harmonics


def step_back(index, j, harmonics):
    if harmonics & (harmonics - 1) == 0:
        return lax.bitwise_xor(index, j)
    return lax.rem(index - j + harmonics, harmonics)


def scales(count, harmonics):
    vector = count * WEIGHT_MAX * BASIS_MAX
    flux = harmonics * FLOW_MAX * vector
    applied = (SHIFT_MAX + 12.0 * VISCOSITY) * vector + DIRS * flux
    return [2.0 ** math.floor(math.log2(SENT_MAX / bound)) for bound in (vector, applied)]


def start_kernel(basis_in, weights_in, flow_in, basis, vec, message, scalars, weights, flow, sems, *, rescale):
    count, fields = basis.shape[0], basis.shape[2]
    copies = [pltpu.make_async_copy(weights_in, weights, sems.at[0])]
    copies.append(pltpu.make_async_copy(flow_in, flow, sems.at[1]))
    copies += [pltpu.make_async_copy(basis_in.at[j], basis.at[j], sems.at[2 + j]) for j in range(count)]
    for copy in copies:
        copy.start()
    for copy in copies:
        copy.wait()
    for f in range(fields):
        total = weights[0] * basis[0, 0, f]
        for j in range(1, count):
            total = total + weights[j] * basis[j, 0, f]
        vec[f] = total
        message[f] = total * rescale
    message[fields:] = flow[0].astype(F32)
    for j in range(count):
        scalars[j : j + 1] = jnp.full((1, scalars.shape[1]), weights[j], F32)


def gram_kernel(basis, sums):
    count = basis.shape[0]
    lanes = lax.broadcasted_iota(jnp.int32, sums.shape, 1)
    line, place = jnp.zeros(sums.shape, F32), 1 + count
    for i in range(count):
        for j in range(i, count):
            line = jnp.where(lanes == place, jnp.sum(basis[i, 0] * basis[j, 0]), line)
            place += 1
    sums[...] = line


def flux_kernel(shift, vec, *refs, harmonics, unscale, rescale):
    messages = refs[:harmonics]
    partial, away, away_sent, flows = refs[harmonics:]
    fields, planes = vec.shape[0], vec.shape[1]
    harm = lax.axis_index("harm")
    core = parity()
    sign = 0.5 * (1 - 2 * core).astype(F32)
    flip = core == 1
    for j in range(harmonics):
        flows[step_back(harm, j, harmonics)] = messages[j][fields:]
    own = shift[...] + 6.0 * VISCOSITY
    for f in range(fields):
        local, plus, minus = [], [], []
        for t in range(planes):
            x = jnp.where(flip, planes - 1 - t, t)
            center = vec[f, x]
            flux = [flows[0, d, x] * center for d in range(DIRS)]
            for j in range(1, harmonics):
                other = messages[j][f, x] * unscale
                row = lax.rem(harm - step_back(harm, j, harmonics) + harmonics, harmonics)
                flux = [flux[d] + flows[row, d, x] * other for d in range(DIRS)]
            half_y = 0.5 * flux[1]
            half_z = 0.5 * flux[2]
            half_x = sign * flux[0]
            value = own * center + y_up(half_y - VISCOSITY * center) - y_down(half_y + VISCOSITY * center)
            value = value + z_up(half_z - VISCOSITY * center) - z_down(half_z + VISCOSITY * center)
            local.append(value)
            plus.append(half_x - VISCOSITY * center)
            minus.append(-half_x - VISCOSITY * center)
        for t in range(planes):
            value = local[t]
            if t + 1 < planes:
                value = value + plus[t + 1]
            if t > 0:
                value = value + minus[t - 1]
            partial[t, f] = value
        partial[planes, f] = minus[planes - 1]
        away[f] = plus[0]
        away_sent[f] = plus[0] * rescale


def chip_kernel(mine, theirs, away, message, *, rescale):
    planes = mine.shape[0] - 1
    for t in range(planes):
        own, other = mine[t], theirs[planes - 1 - t]
        if t == planes - 1:
            own = own + theirs[planes]
        if t == 0:
            other = other + mine[planes]
        message[t] = own * rescale
        message[planes + t] = other * rescale
    message[2 * planes] = away[...] * rescale


def inner_kernel(mine, theirs, away, outer, message, *, unscale):
    planes = mine.shape[0] - 1
    message[0] = outer[0] * unscale + away[...]
    for t in range(1, planes):
        message[t] = outer[t] * unscale
    own = mine[0] + outer[2 * planes] * unscale
    if planes == 1:
        own = own + theirs[planes]
    message[planes] = own


def chebyshev_kernel(shift, gram, basis, vec, mine, theirs, away, outer, inner, far, change, sums, *, unscale):
    count, fields = basis.shape[0], vec.shape[0]
    planes = mine.shape[0] - 1
    slab, slabs = lax.axis_index("slab"), lax.axis_size("slab")
    core = parity()
    flip = core == 1
    chip, chips = lax.div(slab, 2), slabs // 2
    has_low = (chip > 0).astype(F32)
    has_high = (chip < chips - 1).astype(F32)
    has_outer = jnp.where(flip, has_high, has_low)
    has_inner = jnp.where(flip, has_low, has_high)
    two_away = jnp.where(flip, chips - 1 - chip, chip) > 1
    has_far = two_away.astype(F32)
    own_shift = shift[...]
    middle = own_shift + 6.0 * VISCOSITY
    half_span = 6.0 * VISCOSITY
    span_ratio = middle / half_span
    ratio = 1.0 / span_ratio
    gains, far_gain = [], 1.0 / middle
    for _ in range(SWEEPS):
        following = 1.0 / (2.0 * span_ratio - ratio)
        gains.append((following * ratio, 2.0 * following / half_span))
        far_gain = far_gain * (gains[-1][1] * VISCOSITY)
        ratio = following
    depth = SWEEPS
    first = 1.0 / middle
    totals = [None] * (1 + count)
    for f in range(fields):
        remainder = [outer[depth - 1 - i, f] * unscale for i in range(depth - 1)]
        remainder.append(outer[0, f] * unscale + away[f])
        scale = [has_outer] * depth + [None] * (2 * planes) + [has_inner] * planes
        for t in range(planes):
            value = mine[t, f]
            if t == planes - 1:
                value = value + theirs[planes, f]
            if t == 0:
                value = value + outer[2 * planes, f] * unscale
            remainder.append(value)
        for t in range(planes - 1, -1, -1):
            if t == 0:
                remainder.append(inner[planes, f])
            elif t == planes - 1:
                remainder.append(theirs[t, f] + mine[planes, f])
            else:
                remainder.append(theirs[t, f])
        for t in range(planes):
            remainder.append(inner[t, f])
        direction = [
            (r * first) if m is None else (r * (first * m)) for r, m in zip(remainder, scale)
        ]
        solution = [direction[depth + t] for t in range(planes)]
        low = 0
        for sweep in range(SWEEPS):
            keep, gain = gains[sweep]
            nothing = low + 1
            end = low + len(direction) - 1
            next_remainder, next_direction = [], []
            for position in range(nothing, end):
                i = position - low
                d = direction[i]
                around = direction[i + 1] + direction[i - 1] + y_up(d) + y_down(d) + z_up(d) + z_down(d)
                r = remainder[i] - (middle * d - VISCOSITY * around)
                m = scale[position]
                if m is None:
                    n = keep * d + gain * r
                else:
                    n = (keep * m) * d + (gain * m) * r
                next_remainder.append(r)
                next_direction.append(n)
            remainder, direction, low = next_remainder, next_direction, low + 1
            solution = [s + direction[depth - low + t] for t, s in enumerate(solution)]
        solution[0] = solution[0] + (far_gain * unscale * has_far) * far[f]
        for t in range(planes):
            x = jnp.where(flip, planes - 1 - t, t)
            moved = solution[t] - vec[f, x]
            change[f, x] = moved
            parts = [moved * moved] + [basis[j, 0, f, x] * moved for j in range(count)]
            totals = [p if q is None else q + p for q, p in zip(totals, parts)]
    lanes = lax.broadcasted_iota(jnp.int32, (1, sums.shape[-1]), 1)
    line = gram[...]
    place = 0
    for total in totals:
        line = jnp.where(lanes == place, jnp.sum(total), line)
        place += 1
    sums[...] = jnp.broadcast_to(line[None], sums.shape)


def final_kernel(scalars, basis, change, sums, vector, column, *, entries):
    count = basis.shape[0]
    line = jnp.sum(sums[:, 0, :], axis=0, keepdims=True) * (1.0 / entries)
    lanes = lax.broadcasted_iota(jnp.int32, line.shape, 1)

    def entry(place):
        return jnp.sum(jnp.where(lanes == place, line, 0.0), axis=1, keepdims=True)

    square = entry(0)
    moved = [entry(1 + j) for j in range(count)]
    gram, place = {}, 1 + count
    for i in range(count):
        for j in range(i, count):
            gram[i, j] = gram[j, i] = entry(place)
            place += 1
    weights = [scalars[j : j + 1] for j in range(count)]
    projection, excess = [], []
    for j in range(count):
        value = moved[j]
        for i in range(count):
            value = value + weights[i] * gram[i, j]
        projection.append(value)
        excess.append(value - weights[j])
    for j in range(count):
        inner = -2.0 * moved[j]
        for i in range(count):
            inner = inner + excess[i] * gram[i, j]
        square = square + excess[j] * inner
    norm = jnp.sqrt(jnp.maximum(square, 0.0) + EPSILON)
    inverse = (1.0 / norm)[:, None, None, :]
    residue = change[...]
    for j in range(count):
        residue = residue - excess[j][:, None, None, :] * basis[j, 0]
    vector[0] = residue * inverse
    for j in range(count):
        column[j] = jnp.max(projection[j])
    column[count] = jnp.max(norm)


def shards(krylov_basis, weights, base_flow, shifts):
    count, _, fields, planes, ny, nz = krylov_basis.shape
    harmonics, slabs = lax.axis_size("harm"), lax.axis_size("slab")
    assert 2 * planes == SWEEPS and slabs % 2 == 0
    shape = (fields, planes, ny, nz)
    vec_scale, applied_scale = scales(count, harmonics)

    def start_body(*refs):
        start_kernel(*refs, rescale=vec_scale)

    basis, vec, message, scalars = call(
        start_body,
        [
            jax.ShapeDtypeStruct(krylov_basis.shape, F32),
            jax.ShapeDtypeStruct(shape, F32),
            jax.ShapeDtypeStruct((fields + DIRS, planes, ny, nz), F32),
            jax.ShapeDtypeStruct((count, nz), F32),
        ],
        [*(pltpu.with_memory_space_constraint(x, pltpu.HBM) for x in (krylov_basis, weights, base_flow))],
        [pl.BlockSpec(memory_space=pltpu.HBM)] * 3,
        [VMEM] * 4,
        [
            pltpu.SMEM(weights.shape, F32),
            pltpu.VMEM(base_flow.shape, base_flow.dtype),
            pltpu.SemaphoreType.DMA((2 + count,)),
        ],
    )
    whole, message = message, message.astype(SENT)
    shift = jnp.broadcast_to(shifts[:, None], (1, nz))
    gram = call(gram_kernel, jax.ShapeDtypeStruct((1, nz), F32), (basis,), [VMEM], VMEM)
    messages = [whole] + [
        lax.ppermute(message, "harm", [(i, step(i, j, harmonics)) for i in range(harmonics)]).astype(F32)
        for j in range(1, harmonics)
    ]

    def flux_body(*refs):
        flux_kernel(*refs, harmonics=harmonics, unscale=1.0 / vec_scale, rescale=applied_scale)

    mine, away, away_sent = call(
        flux_body,
        [
            jax.ShapeDtypeStruct((planes + 1, fields, ny, nz), F32),
            jax.ShapeDtypeStruct((fields, ny, nz), F32),
            jax.ShapeDtypeStruct((fields, ny, nz), F32),
        ],
        (shift, vec, *messages),
        [VMEM] * (2 + harmonics),
        [VMEM] * 3,
        [pltpu.VMEM((harmonics, DIRS, planes, ny, nz), F32)],
    )
    swap = [(i, i ^ 1) for i in range(slabs)]
    links = [(i, i + 1) for i in range(1, slabs - 1, 2)]
    cross = links + [(b, a) for a, b in links]
    skips = [(i, i + 3) for i in range(1, slabs - 3, 2)]
    beyond = skips + [(b, a) for a, b in skips]
    theirs = lax.ppermute(mine, "slab", swap)

    def chip_body(*refs):
        chip_kernel(*refs, rescale=applied_scale)

    chip = call(
        chip_body,
        jax.ShapeDtypeStruct((2 * planes + 1, fields, ny, nz), F32),
        (mine, theirs, away),
        [VMEM] * 3,
        VMEM,
    )
    outer = lax.ppermute(chip.astype(SENT), "slab", cross).astype(F32)
    masks = {a ^ b for a, b in beyond}
    if len(masks) == 1 and slabs & (slabs - 1) == 0:
        beyond = [(i, i ^ mask) for i in range(slabs) for mask in masks]
    far = lax.ppermute(away_sent.astype(SENT), "slab", beyond).astype(F32)

    def inner_body(*refs):
        inner_kernel(*refs, unscale=1.0 / applied_scale)

    held = call(
        inner_body,
        jax.ShapeDtypeStruct((planes + 1, fields, ny, nz), F32),
        (mine, theirs, away, outer),
        [VMEM] * 4,
        VMEM,
    )
    inner = lax.ppermute(held, "slab", swap)
    devices = harmonics * slabs

    def chebyshev_body(*refs):
        chebyshev_kernel(*refs, unscale=1.0 / applied_scale)

    change, sums = call(
        chebyshev_body,
        [jax.ShapeDtypeStruct(shape, F32), jax.ShapeDtypeStruct((devices, 1, nz), F32)],
        (shift, gram, basis, vec, mine, theirs, away, outer, inner, far),
        [VMEM] * 10,
        [VMEM, VMEM],
    )
    sums = lax.all_to_all(sums, ("harm", "slab"), 0, 0, tiled=True)
    entries = float(devices * fields * planes * ny * nz)

    def final_body(*refs):
        final_kernel(*refs, entries=entries)

    vector, column = call(
        final_body,
        [jax.ShapeDtypeStruct((1,) + shape, F32), jax.ShapeDtypeStruct((count + 1,), F32)],
        (scalars, basis, change, sums),
        [VMEM] * 4,
        [VMEM, SMEM],
    )
    return vector, column


def solution(mesh):
    in_specs = (
        P(None, "harm", None, "slab", None, None),
        P(),
        P("harm", None, "slab", None, None),
        P("harm"),
    )
    out_specs = (P("harm", None, "slab", None, None), P())

    return jax.shard_map(shards, mesh=mesh, in_specs=in_specs, out_specs=out_specs, check_vma=False)
```

```python
import math

import jax
import jax.numpy as jnp
from jax import lax
from jax.experimental import pallas as pl
from jax.experimental.pallas import tpu as pltpu
from jax.sharding import PartitionSpec as P


SWEEPS = 4
DIRS = 3
VISCOSITY = 1.0
EPSILON = 1e-06
BASIS_MAX, WEIGHT_MAX, FLOW_MAX, SHIFT_MAX = 16.0, 3.0, 4.0, 2.0
SENT_MAX = 60000.0
F32 = jnp.float32
SENT = jnp.float16
VMEM = pl.BlockSpec(memory_space=pltpu.VMEM)
SMEM = pl.BlockSpec(memory_space=pltpu.SMEM)


def call(body, out_shape, args, specs, out_specs, scratch=()):
    return pl.pallas_call(
        body, out_shape=out_shape, in_specs=specs, out_specs=out_specs, scratch_shapes=scratch,
        compiler_params=pltpu.CompilerParams(vmem_limit_bytes=8 << 20),
    )(*args)


def rows(shape):
    return lax.broadcasted_iota(jnp.int32, shape, len(shape) - 2)


def y_up(plane):
    count = plane.shape[-2]
    return jnp.where(rows(plane.shape) < count - 1, pltpu.roll(plane, count - 1, plane.ndim - 2), 0.0)


def y_down(plane):
    return jnp.where(rows(plane.shape) > 0, pltpu.roll(plane, 1, plane.ndim - 2), 0.0)


def z_up(plane):
    return pltpu.roll(plane, plane.shape[-1] - 1, plane.ndim - 1)


def z_down(plane):
    return pltpu.roll(plane, 1, plane.ndim - 1)


def parity():
    return lax.rem(lax.axis_index("slab"), 2)


def step(index, j, harmonics):
    if harmonics & (harmonics - 1) == 0:
        return index ^ j
    return (index + j) % harmonics


def step_back(index, j, harmonics):
    if harmonics & (harmonics - 1) == 0:
        return lax.bitwise_xor(index, j)
    return lax.rem(index - j + harmonics, harmonics)


def scales(count, harmonics):
    vector = count * WEIGHT_MAX * BASIS_MAX
    flux = harmonics * FLOW_MAX * vector
    applied = (SHIFT_MAX + 12.0 * VISCOSITY) * vector + DIRS * flux
    return [2.0 ** math.floor(math.log2(SENT_MAX / bound)) for bound in (vector, applied)]


def start_kernel(basis_in, weights_in, flow_in, basis, vec, message, scalars, weights, flow, sems, *, rescale):
    count, fields = basis.shape[0], basis.shape[2]
    copies = [pltpu.make_async_copy(weights_in, weights, sems.at[0])]
    copies.append(pltpu.make_async_copy(flow_in, flow, sems.at[1]))
    copies += [pltpu.make_async_copy(basis_in.at[j], basis.at[j], sems.at[2 + j]) for j in range(count)]
    for copy in copies:
        copy.start()
    for copy in copies:
        copy.wait()
    for f in range(fields):
        total = weights[0] * basis[0, 0, f]
        for j in range(1, count):
            total = total + weights[j] * basis[j, 0, f]
        vec[f] = total
        message[f] = total * rescale
    message[fields:] = flow[0].astype(F32)
    for j in range(count):
        scalars[j : j + 1] = jnp.full((1, scalars.shape[1]), weights[j], F32)


def gram_kernel(basis, sums):
    count = basis.shape[0]
    lanes = lax.broadcasted_iota(jnp.int32, sums.shape, 1)
    line, place = jnp.zeros(sums.shape, F32), 1 + count
    for i in range(count):
        for j in range(i, count):
            line = jnp.where(lanes == place, jnp.sum(basis[i, 0] * basis[j, 0]), line)
            place += 1
    sums[...] = line


def flux_kernel(shift, vec, *refs, harmonics, unscale, rescale):
    messages = refs[:harmonics]
    partial, away, away_sent, flows = refs[harmonics:]
    fields, planes = vec.shape[0], vec.shape[1]
    harm = lax.axis_index("harm")
    core = parity()
    sign = 0.5 * (1 - 2 * core).astype(F32)
    flip = core == 1
    for j in range(harmonics):
        flows[step_back(harm, j, harmonics)] = messages[j][fields:]
    own = shift[...] + 6.0 * VISCOSITY
    for f in range(fields):
        local, plus, minus = [], [], []
        for t in range(planes):
            x = jnp.where(flip, planes - 1 - t, t)
            center = vec[f, x]
            flux = [flows[0, d, x] * center for d in range(DIRS)]
            for j in range(1, harmonics):
                other = messages[j][f, x] * unscale
                row = lax.rem(harm - step_back(harm, j, harmonics) + harmonics, harmonics)
                flux = [flux[d] + flows[row, d, x] * other for d in range(DIRS)]
            half_y = 0.5 * flux[1]
            half_z = 0.5 * flux[2]
            half_x = sign * flux[0]
            value = own * center + y_up(half_y - VISCOSITY * center) - y_down(half_y + VISCOSITY * center)
            value = value + z_up(half_z - VISCOSITY * center) - z_down(half_z + VISCOSITY * center)
            local.append(value)
            plus.append(half_x - VISCOSITY * center)
            minus.append(-half_x - VISCOSITY * center)
        for t in range(planes):
            value = local[t]
            if t + 1 < planes:
                value = value + plus[t + 1]
            if t > 0:
                value = value + minus[t - 1]
            partial[t, f] = value
        partial[planes, f] = minus[planes - 1]
        away[f] = plus[0]
        away_sent[f] = plus[0] * rescale


def chip_kernel(mine, theirs, away, message, *, rescale):
    planes = mine.shape[0] - 1
    for t in range(planes):
        own, other = mine[t], theirs[planes - 1 - t]
        if t == planes - 1:
            own = own + theirs[planes]
        if t == 0:
            other = other + mine[planes]
        message[t] = own * rescale
        message[planes + t] = other * rescale
    message[2 * planes] = away[...] * rescale


def inner_kernel(away, outer, message, *, unscale):
    planes = message.shape[0] - 1
    message[0] = outer[0] * unscale + away[...]
    for t in range(1, planes):
        message[t] = outer[t] * unscale
    message[planes] = outer[2 * planes] * unscale


def neighbours():
    slab, slabs = lax.axis_index("slab"), lax.axis_size("slab")
    flip = parity() == 1
    chip, chips = lax.div(slab, 2), slabs // 2
    before = jnp.where(flip, chips - 1 - chip, chip)
    after = jnp.where(flip, chip, chips - 1 - chip)
    return [x.astype(F32) for x in (before > 0, after > 0, before > 1)]


def recurrence(shift):
    middle = shift + 6.0 * VISCOSITY
    half_span = 6.0 * VISCOSITY
    span_ratio = middle / half_span
    first = 1.0 / middle
    ratio, unit = 1.0 / span_ratio, 1.0
    units, same, past = [], [], []
    kept = gained = None
    for _ in range(SWEEPS):
        following = 1.0 / (2.0 * span_ratio - ratio)
        gain = 2.0 * following / half_span * VISCOSITY
        inverse = 1.0 / gain
        keep = following * ratio * inverse
        if gained is None:
            same.append(keep)
            past.append(None)
        else:
            same.append(keep + gained - middle * (1.0 / VISCOSITY))
            past.append(kept * gained)
        unit = unit * gain
        units.append(unit)
        kept, gained, ratio = keep, inverse, following
    return first, units, same, past


def sweeps(applied, outside, planes, coefficients):
    first, units, same, past = coefficients
    direction = {p: v * first if p not in outside else v * (first * outside[p]) for p, v in applied.items()}
    solution = {t: direction[t] for t in range(planes) if t in direction}
    previous = {}
    for n in range(SWEEPS):
        reach = SWEEPS - 1 - n
        fresh = {}
        for p in range(-reach, planes + reach):
            terms = [direction[q] for q in (p - 1, p + 1) if q in direction]
            if p in direction:
                d = direction[p]
                terms += [y_up(d), y_down(d), z_up(d), z_down(d), same[n] * d]
            if not terms:
                continue
            value = terms[0]
            for term in terms[1:]:
                value = value + term
            if p in previous:
                value = value - past[n] * previous[p]
            fresh[p] = value if p not in outside else outside[p] * value
        previous, direction = direction, fresh
        for t in range(planes):
            if t in direction:
                part = units[n] * direction[t]
                solution[t] = solution[t] + part if t in solution else part
    return solution


def near_kernel(shift, mine, theirs, away, outer, part, *, unscale):
    fields, planes = part.shape[1], part.shape[0]
    has_outer, has_inner, _ = neighbours()
    coefficients = recurrence(shift[...])
    for f in range(fields):
        applied, outside = {}, {2 * planes + t: has_inner for t in range(planes)}
        for i in range(2 * planes):
            value = outer[i, f] * unscale
            applied[-1 - i] = value + away[f] if i == 0 else value
            outside[-1 - i] = has_outer
        for t in range(planes):
            own, other = mine[t, f], theirs[t, f]
            if t == planes - 1:
                own, other = own + theirs[planes, f], other + mine[planes, f]
            if t == 0:
                own = own + outer[2 * planes, f] * unscale
            applied[t] = own
            applied[2 * planes - 1 - t] = other
        solution = sweeps(applied, outside, planes, coefficients)
        for t in range(planes):
            part[t, f] = solution[t]


def chebyshev_kernel(shift, gram, basis, vec, part, inner, far, change, sums, *, unscale):
    count, fields = basis.shape[0], vec.shape[0]
    planes = part.shape[0]
    _, has_inner, has_far = neighbours()
    flip = parity() == 1
    coefficients = recurrence(shift[...])
    far_gain = coefficients[0] * coefficients[1][-1] * (unscale * has_far)
    totals = [None] * (1 + count)
    for f in range(fields):
        applied = {2 * planes - 1: inner[planes, f]}
        outside = {}
        for t in range(planes):
            applied[2 * planes + t] = inner[t, f]
            outside[2 * planes + t] = has_inner
        solution = sweeps(applied, outside, planes, coefficients)
        for t in range(planes):
            x = jnp.where(flip, planes - 1 - t, t)
            value = part[t, f] + solution[t]
            if t == 0:
                value = value + far_gain * far[f]
            moved = value - vec[f, x]
            change[f, x] = moved
            parts = [moved * moved] + [basis[j, 0, f, x] * moved for j in range(count)]
            totals = [p if q is None else q + p for q, p in zip(totals, parts)]
    lanes = lax.broadcasted_iota(jnp.int32, (1, sums.shape[-1]), 1)
    line = gram[...]
    place = 0
    for total in totals:
        line = jnp.where(lanes == place, jnp.sum(total), line)
        place += 1
    sums[...] = jnp.broadcast_to(line[None], sums.shape)


def final_kernel(scalars, basis, change, sums, vector, column, *, entries):
    count = basis.shape[0]
    line = jnp.sum(sums[:, 0, :], axis=0, keepdims=True) * (1.0 / entries)
    lanes = lax.broadcasted_iota(jnp.int32, line.shape, 1)

    def entry(place):
        return jnp.sum(jnp.where(lanes == place, line, 0.0), axis=1, keepdims=True)

    square = entry(0)
    moved = [entry(1 + j) for j in range(count)]
    gram, place = {}, 1 + count
    for i in range(count):
        for j in range(i, count):
            gram[i, j] = gram[j, i] = entry(place)
            place += 1
    weights = [scalars[j : j + 1] for j in range(count)]
    projection, excess = [], []
    for j in range(count):
        value = moved[j]
        for i in range(count):
            value = value + weights[i] * gram[i, j]
        projection.append(value)
        excess.append(value - weights[j])
    for j in range(count):
        inner = -2.0 * moved[j]
        for i in range(count):
            inner = inner + excess[i] * gram[i, j]
        square = square + excess[j] * inner
    norm = jnp.sqrt(jnp.maximum(square, 0.0) + EPSILON)
    inverse = (1.0 / norm)[:, None, None, :]
    residue = change[...]
    for j in range(count):
        residue = residue - excess[j][:, None, None, :] * basis[j, 0]
    vector[0] = residue * inverse
    for j in range(count):
        column[j] = jnp.max(projection[j])
    column[count] = jnp.max(norm)


def shards(krylov_basis, weights, base_flow, shifts):
    count, _, fields, planes, ny, nz = krylov_basis.shape
    harmonics, slabs = lax.axis_size("harm"), lax.axis_size("slab")
    assert 2 * planes == SWEEPS and slabs % 2 == 0
    shape = (fields, planes, ny, nz)
    vec_scale, applied_scale = scales(count, harmonics)

    def start_body(*refs):
        start_kernel(*refs, rescale=vec_scale)

    basis, vec, message, scalars = call(
        start_body,
        [
            jax.ShapeDtypeStruct(krylov_basis.shape, F32),
            jax.ShapeDtypeStruct(shape, F32),
            jax.ShapeDtypeStruct((fields + DIRS, planes, ny, nz), F32),
            jax.ShapeDtypeStruct((count, nz), F32),
        ],
        [*(pltpu.with_memory_space_constraint(x, pltpu.HBM) for x in (krylov_basis, weights, base_flow))],
        [pl.BlockSpec(memory_space=pltpu.HBM)] * 3,
        [VMEM] * 4,
        [
            pltpu.SMEM(weights.shape, F32),
            pltpu.VMEM(base_flow.shape, base_flow.dtype),
            pltpu.SemaphoreType.DMA((2 + count,)),
        ],
    )
    whole, message = message, message.astype(SENT)
    shift = jnp.broadcast_to(shifts[:, None], (1, nz))
    gram = call(gram_kernel, jax.ShapeDtypeStruct((1, nz), F32), (basis,), [VMEM], VMEM)
    messages = [whole] + [
        lax.ppermute(message, "harm", [(i, step(i, j, harmonics)) for i in range(harmonics)]).astype(F32)
        for j in range(1, harmonics)
    ]

    def flux_body(*refs):
        flux_kernel(*refs, harmonics=harmonics, unscale=1.0 / vec_scale, rescale=applied_scale)

    mine, away, away_sent = call(
        flux_body,
        [
            jax.ShapeDtypeStruct((planes + 1, fields, ny, nz), F32),
            jax.ShapeDtypeStruct((fields, ny, nz), F32),
            jax.ShapeDtypeStruct((fields, ny, nz), F32),
        ],
        (shift, vec, *messages),
        [VMEM] * (2 + harmonics),
        [VMEM] * 3,
        [pltpu.VMEM((harmonics, DIRS, planes, ny, nz), F32)],
    )
    swap = [(i, i ^ 1) for i in range(slabs)]
    links = [(i, i + 1) for i in range(1, slabs - 1, 2)]
    cross = links + [(b, a) for a, b in links]
    skips = [(i, i + 3) for i in range(1, slabs - 3, 2)]
    beyond = skips + [(b, a) for a, b in skips]
    theirs = lax.ppermute(mine, "slab", swap)

    def chip_body(*refs):
        chip_kernel(*refs, rescale=applied_scale)

    chip = call(
        chip_body,
        jax.ShapeDtypeStruct((2 * planes + 1, fields, ny, nz), F32),
        (mine, theirs, away),
        [VMEM] * 3,
        VMEM,
    )
    outer = lax.ppermute(chip.astype(SENT), "slab", cross).astype(F32)
    masks = {a ^ b for a, b in beyond}
    if len(masks) == 1 and slabs & (slabs - 1) == 0:
        beyond = [(i, i ^ mask) for i in range(slabs) for mask in masks]
    far = lax.ppermute(away_sent.astype(SENT), "slab", beyond).astype(F32)

    def inner_body(*refs):
        inner_kernel(*refs, unscale=1.0 / applied_scale)

    held = call(
        inner_body,
        jax.ShapeDtypeStruct((planes + 1, fields, ny, nz), F32),
        (away, outer),
        [VMEM] * 2,
        VMEM,
    )
    inner = lax.ppermute(held, "slab", swap)
    devices = harmonics * slabs

    def near_body(*refs):
        near_kernel(*refs, unscale=1.0 / applied_scale)

    part = call(
        near_body,
        jax.ShapeDtypeStruct((planes, fields, ny, nz), F32),
        (shift, mine, theirs, away, outer),
        [VMEM] * 5,
        VMEM,
    )

    def chebyshev_body(*refs):
        chebyshev_kernel(*refs, unscale=1.0 / applied_scale)

    change, sums = call(
        chebyshev_body,
        [jax.ShapeDtypeStruct(shape, F32), jax.ShapeDtypeStruct((devices, 1, nz), F32)],
        (shift, gram, basis, vec, part, inner, far),
        [VMEM] * 7,
        [VMEM, VMEM],
    )
    sums = lax.all_to_all(sums, ("harm", "slab"), 0, 0, tiled=True)
    entries = float(devices * fields * planes * ny * nz)

    def final_body(*refs):
        final_kernel(*refs, entries=entries)

    vector, column = call(
        final_body,
        [jax.ShapeDtypeStruct((1,) + shape, F32), jax.ShapeDtypeStruct((count + 1,), F32)],
        (scalars, basis, change, sums),
        [VMEM] * 4,
        [VMEM, SMEM],
    )
    return vector, column


def solution(mesh):
    in_specs = (
        P(None, "harm", None, "slab", None, None),
        P(),
        P("harm", None, "slab", None, None),
        P("harm"),
    )
    out_specs = (P("harm", None, "slab", None, None), P())

    return jax.shard_map(shards, mesh=mesh, in_specs=in_specs, out_specs=out_specs, check_vma=False)
```

```python
import math

import jax
import jax.numpy as jnp
from jax import lax
from jax.experimental import pallas as pl
from jax.experimental.pallas import tpu as pltpu
from jax.sharding import PartitionSpec as P


SWEEPS = 4
DIRS = 3
VISCOSITY = 1.0
EPSILON = 1e-06
BASIS_MAX, WEIGHT_MAX, FLOW_MAX, SHIFT_MAX = 16.0, 3.0, 4.0, 2.0
SENT_MAX = 60000.0
F32 = jnp.float32
SENT = jnp.float16
VMEM = pl.BlockSpec(memory_space=pltpu.VMEM)
SMEM = pl.BlockSpec(memory_space=pltpu.SMEM)


def call(body, out_shape, args, specs, out_specs, scratch=()):
    return pl.pallas_call(
        body, out_shape=out_shape, in_specs=specs, out_specs=out_specs, scratch_shapes=scratch,
        compiler_params=pltpu.CompilerParams(vmem_limit_bytes=8 << 20),
    )(*args)


def rows(shape):
    return lax.broadcasted_iota(jnp.int32, shape, len(shape) - 2)


def y_up(plane):
    count = plane.shape[-2]
    return jnp.where(rows(plane.shape) < count - 1, pltpu.roll(plane, count - 1, plane.ndim - 2), 0.0)


def y_down(plane):
    return jnp.where(rows(plane.shape) > 0, pltpu.roll(plane, 1, plane.ndim - 2), 0.0)


def z_up(plane):
    return pltpu.roll(plane, plane.shape[-1] - 1, plane.ndim - 1)


def z_down(plane):
    return pltpu.roll(plane, 1, plane.ndim - 1)


def parity():
    return lax.rem(lax.axis_index("slab"), 2)


def step(index, j, harmonics):
    if harmonics & (harmonics - 1) == 0:
        return index ^ j
    return (index + j) % harmonics


def step_back(index, j, harmonics):
    if harmonics & (harmonics - 1) == 0:
        return lax.bitwise_xor(index, j)
    return lax.rem(index - j + harmonics, harmonics)


def scales(count, harmonics):
    vector = count * WEIGHT_MAX * BASIS_MAX
    flux = harmonics * FLOW_MAX * vector
    applied = (SHIFT_MAX + 12.0 * VISCOSITY) * vector + DIRS * flux
    return [2.0 ** math.floor(math.log2(SENT_MAX / bound)) for bound in (vector, FLOW_MAX, applied)]


def start_kernel(basis_in, weights_in, flow_in, basis, vec, message, scalars, weights, flow, sems, *, rescale, flow_rescale):
    count, fields = basis.shape[0], basis.shape[2]
    copies = [pltpu.make_async_copy(weights_in, weights, sems.at[0])]
    copies.append(pltpu.make_async_copy(flow_in, flow, sems.at[1]))
    copies += [pltpu.make_async_copy(basis_in.at[j], basis.at[j], sems.at[2 + j]) for j in range(count)]
    for copy in copies:
        copy.start()
    for copy in copies:
        copy.wait()
    for f in range(fields):
        total = weights[0] * basis[0, 0, f]
        for j in range(1, count):
            total = total + weights[j] * basis[j, 0, f]
        vec[f] = total
        message[f] = total * rescale
    message[fields:] = flow[0].astype(F32) * flow_rescale
    for j in range(count):
        scalars[j : j + 1] = jnp.full((1, scalars.shape[1]), weights[j], F32)


def whole_sum(plane):
    return jnp.sum(jnp.sum(plane, axis=0, keepdims=True), axis=1, keepdims=True)


def gram_kernel(basis, sums):
    count = basis.shape[0]
    lanes = lax.broadcasted_iota(jnp.int32, sums.shape, 1)
    line, place = jnp.zeros(sums.shape, F32), 1 + count
    for i in range(count):
        for j in range(i, count):
            line = jnp.where(lanes == place, whole_sum(jnp.sum(basis[i, 0] * basis[j, 0], axis=(0, 1))), line)
            place += 1
    sums[...] = line


def flux_kernel(shift, vec, *refs, harmonics, unscale, flow_unscale, rescale):
    messages = refs[:harmonics]
    partial, away, away_sent, flows = refs[harmonics:]
    fields, planes = vec.shape[0], vec.shape[1]
    harm = lax.axis_index("harm")
    core = parity()
    sign = 0.5 * (1 - 2 * core).astype(F32)
    flip = core == 1
    for j in range(harmonics):
        flows[step_back(harm, j, harmonics)] = messages[j][fields:]
    own = shift[...] + 6.0 * VISCOSITY
    for f in range(fields):
        local, plus, minus = [], [], []
        for t in range(planes):
            x = jnp.where(flip, planes - 1 - t, t)
            center = vec[f, x]
            scaled = center * flow_unscale
            flux = [flows[0, d, x] * scaled for d in range(DIRS)]
            for j in range(1, harmonics):
                other = messages[j][f, x] * (unscale * flow_unscale)
                row = lax.rem(harm - step_back(harm, j, harmonics) + harmonics, harmonics)
                flux = [flux[d] + flows[row, d, x] * other for d in range(DIRS)]
            half_y = 0.5 * flux[1]
            half_z = 0.5 * flux[2]
            half_x = sign * flux[0]
            value = own * center + y_up(half_y - VISCOSITY * center) - y_down(half_y + VISCOSITY * center)
            value = value + z_up(half_z - VISCOSITY * center) - z_down(half_z + VISCOSITY * center)
            local.append(value)
            plus.append(half_x - VISCOSITY * center)
            minus.append(-half_x - VISCOSITY * center)
        for t in range(planes):
            value = local[t]
            if t + 1 < planes:
                value = value + plus[t + 1]
            if t > 0:
                value = value + minus[t - 1]
            partial[t, f] = value
        partial[planes, f] = minus[planes - 1]
        away[f] = plus[0]
        away_sent[f] = plus[0] * rescale


def chip_kernel(mine, theirs, away, message, *, rescale):
    planes = mine.shape[0] - 1
    for t in range(planes):
        own, other = mine[t], theirs[planes - 1 - t]
        if t == planes - 1:
            own = own + theirs[planes]
        if t == 0:
            other = other + mine[planes]
        message[t] = own * rescale
        message[planes + t] = other * rescale
    message[2 * planes] = away[...] * rescale


def inner_kernel(away, outer, message, *, unscale):
    planes = message.shape[0] - 1
    message[0] = outer[0] * unscale + away[...]
    for t in range(1, planes):
        message[t] = outer[t] * unscale
    message[planes] = outer[2 * planes] * unscale


def neighbours():
    slab, slabs = lax.axis_index("slab"), lax.axis_size("slab")
    flip = parity() == 1
    chip, chips = lax.div(slab, 2), slabs // 2
    before = jnp.where(flip, chips - 1 - chip, chip)
    after = jnp.where(flip, chip, chips - 1 - chip)
    return [x.astype(F32) for x in (before > 0, after > 0, before > 1)]


def recurrence(shift):
    middle = shift + 6.0 * VISCOSITY
    half_span = 6.0 * VISCOSITY
    span_ratio = middle / half_span
    first = 1.0 / middle
    ratio, unit = 1.0 / span_ratio, 1.0
    units, same, past = [], [], []
    kept = gained = None
    for _ in range(SWEEPS):
        following = 1.0 / (2.0 * span_ratio - ratio)
        gain = 2.0 * following / half_span * VISCOSITY
        inverse = 1.0 / gain
        keep = following * ratio * inverse
        if gained is None:
            same.append(keep)
            past.append(None)
        else:
            same.append(keep + gained - middle * (1.0 / VISCOSITY))
            past.append(kept * gained)
        unit = unit * gain
        units.append(unit)
        kept, gained, ratio = keep, inverse, following
    return first, units, same, past


def sweeps(applied, outside, planes, coefficients):
    first, units, same, past = coefficients
    direction = {p: v * first if p not in outside else v * (first * outside[p]) for p, v in applied.items()}
    solution = {t: direction[t] for t in range(planes) if t in direction}
    previous = {}
    for n in range(SWEEPS):
        reach = SWEEPS - 1 - n
        fresh = {}
        for p in range(-reach, planes + reach):
            terms = [direction[q] for q in (p - 1, p + 1) if q in direction]
            if p in direction:
                d = direction[p]
                terms += [y_up(d), y_down(d), z_up(d), z_down(d), same[n] * d]
            if not terms:
                continue
            value = terms[0]
            for term in terms[1:]:
                value = value + term
            if p in previous:
                value = value - past[n] * previous[p]
            fresh[p] = value if p not in outside else outside[p] * value
        previous, direction = direction, fresh
        for t in range(planes):
            if t in direction:
                part = units[n] * direction[t]
                solution[t] = solution[t] + part if t in solution else part
    return solution


def near_kernel(shift, mine, theirs, away, outer, part, *, unscale):
    fields, planes = part.shape[1], part.shape[0]
    has_outer, has_inner, _ = neighbours()
    coefficients = recurrence(shift[...])
    for f in range(fields):
        applied, outside = {}, {2 * planes + t: has_inner for t in range(planes)}
        for i in range(2 * planes):
            value = outer[i, f] * unscale
            applied[-1 - i] = value + away[f] if i == 0 else value
            outside[-1 - i] = has_outer
        for t in range(planes):
            own, other = mine[t, f], theirs[t, f]
            if t == planes - 1:
                own, other = own + theirs[planes, f], other + mine[planes, f]
            if t == 0:
                own = own + outer[2 * planes, f] * unscale
            applied[t] = own
            applied[2 * planes - 1 - t] = other
        solution = sweeps(applied, outside, planes, coefficients)
        for t in range(planes):
            part[t, f] = solution[t]


def chebyshev_kernel(shift, gram, basis, vec, part, inner, far, change, sums, *, unscale):
    count, fields = basis.shape[0], vec.shape[0]
    planes = part.shape[0]
    _, has_inner, has_far = neighbours()
    flip = parity() == 1
    coefficients = recurrence(shift[...])
    far_gain = coefficients[0] * coefficients[1][-1] * (unscale * has_far)
    totals = [None] * (1 + count)
    for f in range(fields):
        applied = {2 * planes - 1: inner[planes, f]}
        outside = {}
        for t in range(planes):
            applied[2 * planes + t] = inner[t, f]
            outside[2 * planes + t] = has_inner
        solution = sweeps(applied, outside, planes, coefficients)
        for t in range(planes):
            x = jnp.where(flip, planes - 1 - t, t)
            value = part[t, f] + solution[t]
            if t == 0:
                value = value + far_gain * far[f]
            moved = value - vec[f, x]
            change[f, x] = moved
            parts = [moved * moved] + [basis[j, 0, f, x] * moved for j in range(count)]
            totals = [p if q is None else q + p for q, p in zip(totals, parts)]
    lanes = lax.broadcasted_iota(jnp.int32, (1, sums.shape[-1]), 1)
    line = gram[...]
    place = 0
    for total in totals:
        line = jnp.where(lanes == place, whole_sum(total), line)
        place += 1
    sums[...] = jnp.broadcast_to(line[None], sums.shape)


def final_kernel(scalars, basis, change, sums, vector, column, *, entries):
    count = basis.shape[0]
    line = jnp.sum(sums[:, 0, :], axis=0, keepdims=True) * (1.0 / entries)
    lanes = lax.broadcasted_iota(jnp.int32, line.shape, 1)

    def entry(place):
        return jnp.sum(jnp.where(lanes == place, line, 0.0), axis=1, keepdims=True)

    square = entry(0)
    moved = [entry(1 + j) for j in range(count)]
    gram, place = {}, 1 + count
    for i in range(count):
        for j in range(i, count):
            gram[i, j] = gram[j, i] = entry(place)
            place += 1
    weights = [scalars[j : j + 1] for j in range(count)]
    projection, excess = [], []
    for j in range(count):
        value = moved[j]
        for i in range(count):
            value = value + weights[i] * gram[i, j]
        projection.append(value)
        excess.append(value - weights[j])
    for j in range(count):
        inner = -2.0 * moved[j]
        for i in range(count):
            inner = inner + excess[i] * gram[i, j]
        square = square + excess[j] * inner
    norm = jnp.sqrt(jnp.maximum(square, 0.0) + EPSILON)
    inverse = (1.0 / norm)[:, None, None, :]
    residue = change[...]
    for j in range(count):
        residue = residue - excess[j][:, None, None, :] * basis[j, 0]
    vector[0] = residue * inverse
    for j in range(count):
        column[j] = jnp.max(projection[j])
    column[count] = jnp.max(norm)


def shards(krylov_basis, weights, base_flow, shifts):
    count, _, fields, planes, ny, nz = krylov_basis.shape
    harmonics, slabs = lax.axis_size("harm"), lax.axis_size("slab")
    assert 2 * planes == SWEEPS and slabs % 2 == 0
    shape = (fields, planes, ny, nz)
    vec_scale, flow_scale, applied_scale = scales(count, harmonics)

    def start_body(*refs):
        start_kernel(*refs, rescale=vec_scale, flow_rescale=flow_scale)

    basis, vec, message, scalars = call(
        start_body,
        [
            jax.ShapeDtypeStruct(krylov_basis.shape, F32),
            jax.ShapeDtypeStruct(shape, F32),
            jax.ShapeDtypeStruct((fields + DIRS, planes, ny, nz), F32),
            jax.ShapeDtypeStruct((count, nz), F32),
        ],
        [*(pltpu.with_memory_space_constraint(x, pltpu.HBM) for x in (krylov_basis, weights, base_flow))],
        [pl.BlockSpec(memory_space=pltpu.HBM)] * 3,
        [VMEM] * 4,
        [
            pltpu.SMEM(weights.shape, F32),
            pltpu.VMEM(base_flow.shape, base_flow.dtype),
            pltpu.SemaphoreType.DMA((2 + count,)),
        ],
    )
    whole, message = message, message.astype(SENT)
    shift = jnp.broadcast_to(shifts[:, None], (1, nz))
    gram = call(gram_kernel, jax.ShapeDtypeStruct((1, nz), F32), (basis,), [VMEM], VMEM)
    messages = [whole] + [
        lax.ppermute(message, "harm", [(i, step(i, j, harmonics)) for i in range(harmonics)]).astype(F32)
        for j in range(1, harmonics)
    ]

    def flux_body(*refs):
        flux_kernel(*refs, harmonics=harmonics, unscale=1.0 / vec_scale, flow_unscale=1.0 / flow_scale, rescale=applied_scale)

    mine, away, away_sent = call(
        flux_body,
        [
            jax.ShapeDtypeStruct((planes + 1, fields, ny, nz), F32),
            jax.ShapeDtypeStruct((fields, ny, nz), F32),
            jax.ShapeDtypeStruct((fields, ny, nz), F32),
        ],
        (shift, vec, *messages),
        [VMEM] * (2 + harmonics),
        [VMEM] * 3,
        [pltpu.VMEM((harmonics, DIRS, planes, ny, nz), F32)],
    )
    swap = [(i, i ^ 1) for i in range(slabs)]
    links = [(i, i + 1) for i in range(1, slabs - 1, 2)]
    cross = links + [(b, a) for a, b in links]
    skips = [(i, i + 3) for i in range(1, slabs - 3, 2)]
    beyond = skips + [(b, a) for a, b in skips]
    theirs = lax.ppermute(mine, "slab", swap)

    def chip_body(*refs):
        chip_kernel(*refs, rescale=applied_scale)

    chip = call(
        chip_body,
        jax.ShapeDtypeStruct((2 * planes + 1, fields, ny, nz), F32),
        (mine, theirs, away),
        [VMEM] * 3,
        VMEM,
    )
    outer = lax.ppermute(chip.astype(SENT), "slab", cross).astype(F32)
    masks = {a ^ b for a, b in beyond}
    if len(masks) == 1 and slabs & (slabs - 1) == 0:
        beyond = [(i, i ^ mask) for i in range(slabs) for mask in masks]
    far = lax.ppermute(away_sent.astype(SENT), "slab", beyond).astype(F32)

    def inner_body(*refs):
        inner_kernel(*refs, unscale=1.0 / applied_scale)

    held = call(
        inner_body,
        jax.ShapeDtypeStruct((planes + 1, fields, ny, nz), F32),
        (away, outer),
        [VMEM] * 2,
        VMEM,
    )
    inner = lax.ppermute(held, "slab", swap)
    devices = harmonics * slabs

    def near_body(*refs):
        near_kernel(*refs, unscale=1.0 / applied_scale)

    part = call(
        near_body,
        jax.ShapeDtypeStruct((planes, fields, ny, nz), F32),
        (shift, mine, theirs, away, outer),
        [VMEM] * 5,
        VMEM,
    )

    def chebyshev_body(*refs):
        chebyshev_kernel(*refs, unscale=1.0 / applied_scale)

    change, sums = call(
        chebyshev_body,
        [jax.ShapeDtypeStruct(shape, F32), jax.ShapeDtypeStruct((devices, 1, nz), F32)],
        (shift, gram, basis, vec, part, inner, far),
        [VMEM] * 7,
        [VMEM, VMEM],
    )
    sums = lax.all_to_all(sums, ("harm", "slab"), 0, 0, tiled=True)
    entries = float(devices * fields * planes * ny * nz)

    def final_body(*refs):
        final_kernel(*refs, entries=entries)

    vector, column = call(
        final_body,
        [jax.ShapeDtypeStruct((1,) + shape, F32), jax.ShapeDtypeStruct((count + 1,), F32)],
        (scalars, basis, change, sums),
        [VMEM] * 4,
        [VMEM, SMEM],
    )
    return vector, column


def solution(mesh):
    in_specs = (
        P(None, "harm", None, "slab", None, None),
        P(),
        P("harm", None, "slab", None, None),
        P("harm"),
    )
    out_specs = (P("harm", None, "slab", None, None), P())

    return jax.shard_map(shards, mesh=mesh, in_specs=in_specs, out_specs=out_specs, check_vma=False)
```
